32 devices in a mesh: groups: 2 (over y), tensor: 4 (over z), dp: 4 (over x, core).
Axes of the slice: x: 2, y: 2, z: 4, core: 2. Of those that a mesh axis runs over, the one named last changes fastest.
Arguments:
- tokens: bfloat16 [256, 8192], P(('groups', 'tensor', 'dp')), parts along dimension 0, may hold values from -6 to 6
- gate_projection_matrix: bfloat16 [8192, 14336], P('dp', 'tensor'), may hold values from -0.0625 to 0.0625
- up_projection_matrix: bfloat16 [8192, 14336], P('dp', 'tensor'), may hold values from -0.0625 to 0.0625
- down_projection_matrix: bfloat16 [14336, 8192], P('tensor', 'dp'), may hold values from -0.046875 to 0.046875
- gate_adapter_inmap: bfloat16 [16384, 64], P(('groups', 'dp')), parts along dimension 0, may hold values from -0.0625 to 0.0625
- gate_adapter_outmap: bfloat16 [64, 28672], P(None, ('groups', 'tensor')), parts along dimension 1, may hold values from -0.75 to 0.75
- up_adapter_inmap: bfloat16 [16384, 64], P(('groups', 'dp')), parts along dimension 0, may hold values from -0.0625 to 0.0625
- up_adapter_outmap: bfloat16 [64, 28672], P(None, ('groups', 'tensor')), parts along dimension 1, may hold values from -0.75 to 0.75
- down_adapter_inmap: bfloat16 [28672, 64], P(('groups', 'tensor')), parts along dimension 0, may hold values from -0.046875 to 0.046875
- down_adapter_outmap: bfloat16 [64, 16384], P(None, 'groups'), parts along dimension 1, may hold values from -0.75 to 0.75
Outputs:
- block_out: bfloat16 [256, 8192], P(('groups', 'tensor', 'dp')), parts along dimension 0
The draws below stay inside these ranges and needn't reach their ends.
There are 2 independent parts, one for each index of `groups`. The reference program is written for one: setup_inputs(seed, part) draws one part's arguments, and reference() takes and returns one part's arrays. A program takes and returns all parts, laid end to end along the dimension named above; an argument that names none is the same for every part. Nothing has to cross between parts.
All inputs are finite; a program needn't handle non-finite values.
Results may differ from the reference program's by a relative error of at most 0.0053.
Values may be sent and summed in bfloat16 or wider, within the bound.
A program may use at most 256 MiB of HBM per device.

```python
import jax
import jax.numpy as jnp
from jax import lax

MODEL_WIDTH = 8192
HIDDEN_UNITS = 14336
ADAPTER_RANK = 64
TOKENS = 128


def steps_of(stream_key, shape, split, smallest, top_value):
    loudness = 1.0
    for position, blocks in split:
        draws = jax.random.uniform(jax.random.fold_in(jax.random.fold_in(stream_key, 6), position), (blocks,), jnp.float32, smallest / len(split), top_value / len(split))
        loudness = loudness * jnp.repeat(jnp.exp(draws), shape[position] // blocks).reshape((-1,) + (1,) * (len(shape) - 1 - position))
    return loudness


def noise(stream_key, shape, width, reach, shards=(), held_as=jnp.bfloat16):
    gain = steps_of(stream_key, shape, shards, -0.22, 0.18) if shards else 1.0
    result = jax.random.normal(stream_key, shape, jnp.float32) * width * gain
    return jnp.minimum(jnp.maximum(result, -reach), reach).astype(held_as)


def setup_inputs(seed: int = 0, part: int = 0) -> dict:
    keys = jax.random.split(jax.random.key(seed), 11)
    own_keys = jax.random.split(jax.random.fold_in(keys[10], part), 11)
    tokens = noise(own_keys[0], (TOKENS, MODEL_WIDTH), 1.0, 6.0, ((0, 16),))
    gate_projection_matrix = noise(keys[1], (MODEL_WIDTH, HIDDEN_UNITS), MODEL_WIDTH ** -0.5, 0.0625, ((0, 4), (1, 4)))
    up_projection_matrix = noise(keys[2], (MODEL_WIDTH, HIDDEN_UNITS), MODEL_WIDTH ** -0.5, 0.0625, ((0, 4), (1, 4)))
    down_projection_matrix = noise(keys[3], (HIDDEN_UNITS, MODEL_WIDTH), HIDDEN_UNITS ** -0.5, 0.046875, ((0, 4), (1, 4)))
    gate_adapter_inmap = noise(own_keys[4], (MODEL_WIDTH, ADAPTER_RANK), MODEL_WIDTH ** -0.5, 0.0625, ((0, 4),))
    gate_adapter_outmap = noise(own_keys[5], (ADAPTER_RANK, HIDDEN_UNITS), ADAPTER_RANK ** -0.5, 0.75, ((1, 4),))
    up_adapter_inmap = noise(own_keys[6], (MODEL_WIDTH, ADAPTER_RANK), MODEL_WIDTH ** -0.5, 0.0625, ((0, 4),))
    up_adapter_outmap = noise(own_keys[7], (ADAPTER_RANK, HIDDEN_UNITS), ADAPTER_RANK ** -0.5, 0.75, ((1, 4),))
    down_adapter_inmap = noise(own_keys[8], (HIDDEN_UNITS, ADAPTER_RANK), HIDDEN_UNITS ** -0.5, 0.046875, ((0, 4),))
    down_adapter_outmap = noise(own_keys[9], (ADAPTER_RANK, MODEL_WIDTH), ADAPTER_RANK ** -0.5, 0.75)
    return dict(tokens=tokens, gate_projection_matrix=gate_projection_matrix, up_projection_matrix=up_projection_matrix, down_projection_matrix=down_projection_matrix, gate_adapter_inmap=gate_adapter_inmap, gate_adapter_outmap=gate_adapter_outmap, up_adapter_inmap=up_adapter_inmap, up_adapter_outmap=up_adapter_outmap, down_adapter_inmap=down_adapter_inmap, down_adapter_outmap=down_adapter_outmap)


adapter_scale_factor = 0.5


def reference(tokens, gate_projection_matrix, up_projection_matrix, down_projection_matrix, gate_adapter_inmap, gate_adapter_outmap, up_adapter_inmap, up_adapter_outmap, down_adapter_inmap, down_adapter_outmap):
    gate_lowrank_part = jnp.dot(tokens, gate_adapter_inmap, preferred_element_type=jnp.float32).astype(jnp.bfloat16)
    up_lowrank_part = jnp.dot(tokens, up_adapter_inmap, preferred_element_type=jnp.float32).astype(jnp.bfloat16)
    gate_activated = jnp.dot(tokens, gate_projection_matrix, preferred_element_type=jnp.float32) + adapter_scale_factor * jnp.dot(gate_lowrank_part, gate_adapter_outmap, preferred_element_type=jnp.float32)
    up_projected_value = jnp.dot(tokens, up_projection_matrix, preferred_element_type=jnp.float32) + adapter_scale_factor * jnp.dot(up_lowrank_part, up_adapter_outmap, preferred_element_type=jnp.float32)
    hidden_product = (jax.nn.silu(gate_activated) * up_projected_value).astype(jnp.bfloat16)
    down_lowrank_part = jnp.dot(hidden_product, down_adapter_inmap, preferred_element_type=jnp.float32)
    block_result_rows = jnp.dot(hidden_product, down_projection_matrix, preferred_element_type=jnp.float32)
    block_result_rows = block_result_rows + adapter_scale_factor * jnp.dot(down_lowrank_part, down_adapter_outmap.astype(jnp.float32), precision=lax.Precision.HIGHEST)
    return block_result_rows.astype(jnp.bfloat16)
```

```python
import jax
import jax.numpy as jnp
from jax import lax
from jax.sharding import PartitionSpec as P

adapter_scale_factor = 0.5


def body(
    tokens,
    gate_projection_matrix,
    up_projection_matrix,
    down_projection_matrix,
    gate_adapter_inmap,
    gate_adapter_outmap,
    up_adapter_inmap,
    up_adapter_outmap,
    down_adapter_inmap,
    down_adapter_outmap,
):
    adapter_rank_size = gate_adapter_inmap.shape[1]
    columns = lax.all_to_all(tokens, "dp", split_axis=1, concat_axis=0, tiled=True)
    gathered = lax.all_gather(columns, "tensor", axis=0, tiled=True)

    def summed(weights):
        partial = jnp.dot(gathered, weights, preferred_element_type=jnp.float32)
        return lax.psum_scatter(partial, "dp", scatter_dimension=0, tiled=True)

    gate_dense_part = summed(gate_projection_matrix)
    up_dense_part = summed(up_projection_matrix)
    lowrank = summed(jnp.concatenate([gate_adapter_inmap, up_adapter_inmap], axis=1)).astype(
        jnp.bfloat16
    )
    gate_lowrank_part = lowrank[:, :adapter_rank_size]
    up_lowrank_part = lowrank[:, adapter_rank_size:]
    gate_activated = gate_dense_part + adapter_scale_factor * jnp.dot(
        gate_lowrank_part, gate_adapter_outmap, preferred_element_type=jnp.float32
    )
    up_projected_value = up_dense_part + adapter_scale_factor * jnp.dot(
        up_lowrank_part, up_adapter_outmap, preferred_element_type=jnp.float32
    )
    hidden_product = (jax.nn.silu(gate_activated) * up_projected_value).astype(jnp.bfloat16)
    hidden_all = lax.all_gather(hidden_product, "dp", axis=0, tiled=True)
    low = jnp.dot(hidden_all, down_adapter_inmap, preferred_element_type=jnp.float32)
    width = down_projection_matrix.shape[1]
    own_map = lax.dynamic_slice_in_dim(
        down_adapter_outmap, lax.axis_index("dp") * width, width, axis=1
    ).astype(jnp.float32)
    term = jnp.dot(hidden_all, down_projection_matrix, preferred_element_type=jnp.float32)
    term = term + adapter_scale_factor * jnp.dot(low, own_map, precision=lax.Precision.HIGHEST)
    rows_out = lax.psum_scatter(term, "tensor", scatter_dimension=0, tiled=True)
    return lax.all_to_all(
        rows_out.astype(jnp.bfloat16), "dp", split_axis=0, concat_axis=1, tiled=True
    )


def solution(mesh):
    placed = (
        P(("groups", "tensor", "dp"), None),
        P("dp", "tensor"),
        P("dp", "tensor"),
        P("tensor", "dp"),
        P(("groups", "dp"), None),
        P(None, ("groups", "tensor")),
        P(("groups", "dp"), None),
        P(None, ("groups", "tensor")),
        P(("groups", "tensor"), None),
        P(None, "groups"),
    )
    return jax.shard_map(
        body,
        mesh=mesh,
        in_specs=placed,
        out_specs=P(("groups", "tensor", "dp"), None),
        check_vma=False,
    )
```

```python
import functools

import jax
import jax.numpy as jnp
from jax import lax
from jax.experimental import pallas as pl
from jax.experimental.pallas import tpu as pltpu
from jax.sharding import PartitionSpec as P

adapter_scale_factor = 0.5
MESH = pl.DeviceIdType.MESH
SUM_LAG, ACT_LAG, FWD_LAG, DOWN_LAG = 1, 2, 3, 4
SLOTS = ACT_LAG + 1


def kernel(
    nt, nd, nc,
    tok, wg, wu, wd, ag, go, au, uo, di, do, out,
    xbuf, x, wgv, wuv, wdv, agv, auv, gov, uov, div, dov,
    lowp, lowr, lowb, part, send_a, recv_a, send_b, recv_b, hid, acc, dl,
    osend, orecv, fin,
    wsem, ssem, tok_s, tok_r, low_s, low_r, a_s, a_r, b_s, b_r,
    h_s, h_r, p_s, p_r, f_s, f_r, o_s, o_r, z_s, z_r,
):
    n = nt * nd
    half = nd // 2
    depth = wg.shape[0]
    chunk = wgv.shape[2]
    width = wd.shape[1]
    tok_dev = tok.shape[0]
    total_rows = n * tok_dev
    rows = total_rows // nd
    block = nd * tok_dev
    my_t = lax.axis_index("tensor")
    my_d = lax.axis_index("dp")
    me = my_t * nd + my_d
    my_j = lax.div(my_d, 2)
    my_b = lax.rem(my_d, 2)
    other_b = 1 - my_b
    mate = my_j * 2 + other_b

    small = [
        pltpu.make_async_copy(tok.at[:, pl.ds(pl.multiple_of(my_d * depth, 128), depth)], xbuf.at[me], ssem.at[0]),
        pltpu.make_async_copy(ag, agv, ssem.at[1]),
        pltpu.make_async_copy(au, auv, ssem.at[2]),
        pltpu.make_async_copy(do.at[:, pl.ds(pl.multiple_of(my_d * width, 128), width)], dov, ssem.at[3]),
    ]

    def cols(ref, c):
        return ref.at[:, c * chunk : (c + 1) * chunk]

    def rows_of(ref, c):
        return ref.at[c * chunk : (c + 1) * chunk, :]

    plan = (
        (wg, wgv, cols), (wu, wuv, cols), (go, gov, cols), (uo, uov, cols),
        (wd, wdv, rows_of), (di, div, rows_of),
    )

    def load(kind, static_c, c):
        src, dst, cut = plan[kind]
        return pltpu.make_async_copy(cut(src, static_c), dst.at[c], wsem.at[kind, c])

    for copy in small[:3]:
        copy.start()
    for c in range(nc):
        for kind in range(4):
            load(kind, c, c).start()
    small[3].start()
    for c in range(nc):
        for kind in range(4, 6):
            load(kind, c, c).start()

    barrier = pltpu.get_barrier_semaphore()

    def place(index):
        return {"tensor": lax.div(index, nd), "dp": lax.rem(index, nd)}

    def greet(k, carry):
        pl.semaphore_signal(
            barrier, inc=1, device_id=place(lax.rem(me + k, n)), device_id_type=MESH
        )
        return carry

    lax.fori_loop(1, n, greet, 0)
    pl.semaphore_wait(barrier, n - 1)

    def remote(src, dst, send_sem, recv_sem, device):
        return pltpu.make_async_remote_copy(
            src_ref=src, dst_ref=dst, send_sem=send_sem, recv_sem=recv_sem,
            device_id=device, device_id_type=MESH,
        )

    def tok_copy(k):
        index = lax.rem(me + k, n)
        first = pl.multiple_of(lax.rem(index, nd) * depth, 128)
        return remote(
            tok.at[:, pl.ds(first, depth)], xbuf.at[me],
            tok_s.at[k - 1], tok_r.at[k - 1], place(index),
        )

    def each(low, high, act):
        def step(k, carry):
            act(k)
            return carry

        lax.fori_loop(low, high, step, 0)

    each(1, n, lambda k: tok_copy(k).start())
    small[0].wait()
    each(1, n, lambda k: tok_copy(k).wait_recv())
    x[...] = xbuf[...].astype(jnp.float32).reshape(total_rows, depth).astype(jnp.bfloat16)

    small[1].wait()
    small[2].wait()
    for which, ref in ((0, agv), (1, auv)):
        low = jnp.dot(x[...], ref[...], preferred_element_type=jnp.float32)
        for d in range(nd):
            lowp[d, which] = low[d * rows : (d + 1) * rows]

    def low_copy(k):
        d = lax.rem(my_d + k, nd)
        return remote(
            lowp.at[d], lowr.at[k - 1], low_s.at[k - 1], low_r.at[k - 1],
            {"tensor": my_t, "dp": d},
        )

    for k in range(1, nd):
        low_copy(k).start()

    def at_dp(d):
        return {"tensor": my_t, "dp": d}

    def a_copy(c):
        return remote(send_a.at[c], recv_a.at[c], a_s.at[c], a_r.at[c], at_dp(mate))

    def ahead(k):
        return lax.rem(my_j + k, half)

    def behind(k):
        return lax.rem(my_j + half - k, half) * 2 + my_b

    def b_copy(c, k):
        return remote(
            send_b.at[c, k - 1], recv_b.at[c, k - 1],
            b_s.at[c, k - 1], b_r.at[c, k - 1], at_dp(ahead(k) * 2 + my_b),
        )

    def h_copy(c, k):
        return remote(
            hid.at[c, my_d], hid.at[c, my_d],
            h_s.at[c, k - 1], h_r.at[c, k - 1], at_dp(ahead(k) * 2 + my_b),
        )

    def p_copy(c):
        return remote(hid.at[c, my_d], hid.at[c, my_d], p_s.at[c], p_r.at[c], at_dp(mate))

    def f_copy(c, k):
        return remote(
            hid.at[c, behind(k)], hid.at[c, behind(k)],
            f_s.at[c, k - 1], f_r.at[c, k - 1], at_dp(mate),
        )

    def rows_at(d):
        return pl.ds(pl.multiple_of(d * rows, rows), rows)

    def up_part(c):
        load(0, 0, c).wait()
        load(1, 0, c).wait()
        slot = lax.rem(c, SLOTS)
        part[slot, 0] = jnp.dot(x[...], wgv[c], preferred_element_type=jnp.float32)
        part[slot, 1] = jnp.dot(x[...], wuv[c], preferred_element_type=jnp.float32)
        for j in range(half):
            for which in range(2):
                send_a[c, j, which] = part[slot, which, rows_at(2 * j + other_b), :].astype(jnp.bfloat16)
        a_copy(c).start()

    def pair_sum(c):
        a_copy(c).wait_recv()
        slot = lax.rem(c, SLOTS)
        for k in range(1, half):
            j = ahead(k)
            for which in range(2):
                send_b[c, k - 1, which] = (
                    part[slot, which, rows_at(2 * j + my_b), :]
                    + recv_a[c, j, which].astype(jnp.float32)
                ).astype(jnp.bfloat16)
            b_copy(c, k).start()

    def activate(c):
        @pl.when(c == 0)
        def _():
            for k in range(1, nd):
                low_copy(k).wait_recv()
            total = lowp[my_d]
            for k in range(1, nd):
                total = total + lowr[k - 1]
            lowb[...] = total.astype(jnp.bfloat16)

        load(2, 0, c).wait()
        load(3, 0, c).wait()
        slot = lax.rem(c, SLOTS)
        for k in range(1, half):
            b_copy(c, k).wait_recv()
        sums = []
        for which, ref in ((0, gov), (1, uov)):
            value = part[slot, which, rows_at(my_d), :] + recv_a[c, my_j, which].astype(jnp.float32)
            for k in range(1, half):
                value = value + recv_b[c, k - 1, which].astype(jnp.float32)
            value = value + adapter_scale_factor * jnp.dot(
                lowb[which], ref[c], preferred_element_type=jnp.float32
            )
            sums.append(value)
        gate, up = sums
        hid[c, my_d] = (gate / (1.0 + jnp.exp(-gate)) * up).astype(jnp.bfloat16)
        for k in range(1, half):
            h_copy(c, k).start()
        p_copy(c).start()

    def forward(c):
        for k in range(1, half):
            h_copy(c, k).wait_recv()
            f_copy(c, k).start()

    def down_part(c):
        load(4, 0, c).wait()
        load(5, 0, c).wait()
        p_copy(c).wait_recv()
        for k in range(1, half):
            f_copy(c, k).wait_recv()
        lhs = hid[c].reshape(total_rows, chunk)

        @pl.when(c == 0)
        def _():
            acc[...] = jnp.zeros_like(acc)
            dl[...] = jnp.zeros_like(dl)

        step = 512 if width % 512 == 0 else width
        for first in range(0, width, step):
            acc[:, first : first + step] += jnp.dot(
                lhs, wdv[c, :, first : first + step], preferred_element_type=jnp.float32
            )
        dl[...] += jnp.dot(lhs, div[c], preferred_element_type=jnp.float32)

    stages = ((up_part, 0), (pair_sum, SUM_LAG), (activate, ACT_LAG), (forward, FWD_LAG), (down_part, DOWN_LAG))

    def turn(i, carry):
        for stage, lag in stages:
            c = i - lag
            pl.when(jnp.logical_and(c >= 0, c < nc))(functools.partial(stage, c))
        return carry

    lax.fori_loop(0, nc + DOWN_LAG, turn, 0)

    small[3].wait()
    low = dl[...]
    high = low.astype(jnp.bfloat16)
    rest = low - high.astype(jnp.float32)
    middle = rest.astype(jnp.bfloat16)
    last = (rest - middle.astype(jnp.float32)).astype(jnp.bfloat16)
    step = 512 if width % 512 == 0 else width
    for first in range(0, width, step):
        maps = dov[:, first : first + step]
        acc[:, first : first + step] += adapter_scale_factor * (
            jnp.dot(high, maps, preferred_element_type=jnp.float32)
            + (
                jnp.dot(middle, maps, preferred_element_type=jnp.float32)
                + jnp.dot(last, maps, preferred_element_type=jnp.float32)
            )
        )

    def block_at(t):
        return pl.ds(pl.multiple_of(t * block, block), block)

    def o_copy(k):
        t = lax.rem(my_t + k, nt)
        return remote(
            osend.at[k - 1], orecv.at[k - 1], o_s.at[k - 1], o_r.at[k - 1],
            {"tensor": t, "dp": my_d},
        )

    def o_send(k):
        osend[k - 1] = acc[block_at(lax.rem(my_t + k, nt)), :].astype(jnp.bfloat16)
        o_copy(k).start()

    each(1, nt, o_send)

    def o_take(k):
        o_copy(k).wait_recv()
        acc[block_at(my_t), :] += orecv[k - 1].astype(jnp.float32)

    each(1, nt, o_take)
    fin[...] = acc[block_at(my_t), :].reshape(nd, tok_dev, width).astype(jnp.bfloat16)
    mine = pl.ds(pl.multiple_of(my_d * width, 128), width)

    def z_copy(k):
        d = lax.rem(my_d + k, nd)
        return remote(fin.at[d], out.at[:, mine], z_s.at[k - 1], z_r.at[k - 1], at_dp(d))

    def z_wait(k):
        d = lax.rem(my_d + nd - k, nd)
        place_of = pl.ds(pl.multiple_of(d * width, 128), width)
        remote(fin.at[d], out.at[:, place_of], z_s.at[k - 1], z_r.at[k - 1], at_dp(d)).wait_recv()

    for k in range(1, nd):
        z_copy(k).start()
    out[:, mine] = fin[my_d]

    each(1, n, lambda k: tok_copy(k).wait_send())
    for k in range(1, nd):
        low_copy(k).wait_send()

    def drain(c, carry):
        a_copy(c).wait_send()
        p_copy(c).wait_send()
        for k in range(1, half):
            b_copy(c, k).wait_send()
            h_copy(c, k).wait_send()
            f_copy(c, k).wait_send()
        return carry

    lax.fori_loop(0, nc, drain, 0)
    each(1, nt, lambda k: o_copy(k).wait_send())
    for k in range(1, nd):
        z_wait(k)
        z_copy(k).wait_send()


def body(tok, wg, wu, wd, ag, go, au, uo, di, do):
    nt = lax.axis_size("tensor")
    nd = lax.axis_size("dp")
    n = nt * nd
    half = nd // 2
    tok_dev = tok.shape[0]
    depth, hidden = wg.shape
    width = wd.shape[1]
    rank = ag.shape[1]
    chunk = 512 if hidden % 512 == 0 else hidden
    nc = hidden // chunk
    total = n * tok_dev
    rows = total // nd
    block = nd * tok_dev
    far = half - 1
    bf, f32 = jnp.bfloat16, jnp.float32
    vm, dma = pltpu.VMEM, pltpu.SemaphoreType.DMA
    scratch = [
        vm((n, tok_dev, depth), bf), vm((total, depth), bf),
        vm((nc, depth, chunk), bf), vm((nc, depth, chunk), bf), vm((nc, chunk, width), bf),
        vm((depth, rank), bf), vm((depth, rank), bf),
        vm((nc, rank, chunk), bf), vm((nc, rank, chunk), bf), vm((nc, chunk, rank), bf),
        vm((rank, width), bf),
        vm((nd, 2, rows, rank), f32), vm((nd - 1, 2, rows, rank), f32), vm((2, rows, rank), bf),
        vm((SLOTS, 2, total, chunk), f32),
        vm((nc, half, 2, rows, chunk), bf), vm((nc, half, 2, rows, chunk), bf),
        vm((nc, far, 2, rows, chunk), bf), vm((nc, far, 2, rows, chunk), bf),
        vm((nc, nd, rows, chunk), bf),
        vm((total, width), f32), vm((total, rank), f32),
        vm((nt - 1, block, width), bf), vm((nt - 1, block, width), bf), vm((nd, tok_dev, width), bf),
        dma((6, nc)), dma((4,)), dma((n - 1,)), dma((n - 1,)), dma((nd - 1,)), dma((nd - 1,)),
        dma((nc,)), dma((nc,)), dma((nc, far)), dma((nc, far)),
        dma((nc, far)), dma((nc, far)), dma((nc,)), dma((nc,)), dma((nc, far)), dma((nc, far)),
        dma((nt - 1,)), dma((nt - 1,)), dma((nd - 1,)), dma((nd - 1,)),
    ]
    return pl.pallas_call(
        functools.partial(kernel, nt, nd, nc),
        out_shape=jax.ShapeDtypeStruct((tok_dev, width * nd), bf),
        in_specs=[pl.BlockSpec(memory_space=pl.ANY)] * 10,
        out_specs=pl.BlockSpec(memory_space=pltpu.VMEM),
        scratch_shapes=scratch,
        compiler_params=pltpu.CompilerParams(
            collective_id=0, has_side_effects=True, vmem_limit_bytes=67043328
        ),
    )(tok, wg, wu, wd, ag, go, au, uo, di, do)


def solution(mesh):
    placed = (
        P(("groups", "tensor", "dp"), None),
        P("dp", "tensor"),
        P("dp", "tensor"),
        P("tensor", "dp"),
        P(("groups", "dp"), None),
        P(None, ("groups", "tensor")),
        P(("groups", "dp"), None),
        P(None, ("groups", "tensor")),
        P(("groups", "tensor"), None),
        P(None, "groups"),
    )
    return jax.shard_map(
        body,
        mesh=mesh,
        in_specs=placed,
        out_specs=P(("groups", "tensor", "dp"), None),
        check_vma=False,
    )
```

```python
import functools

import jax
import jax.numpy as jnp
from jax import lax
from jax.experimental import pallas as pl
from jax.experimental.pallas import tpu as pltpu
from jax.sharding import PartitionSpec as P

adapter_scale_factor = 0.5
MESH = pl.DeviceIdType.MESH
HALVES = 2
SUM_LAG, ACT_LAG, FWD_LAG, DOWN_LAG = 2, 7, 12, 14


def dot_rows(a, b):
    return lax.dot_general(a, b, (((1,), (1,)), ((), ())), preferred_element_type=jnp.float32)


def kernel(
    nt, nd, nc,
    tok, wg, wu, wd, ag, go, au, uo, di, do, out,
    xbuf, x, wgv, wuv, wdv, agv, auv, gov, uov, div, dov,
    lowp, lowr, lowb, part, send_a, recv_a, send_b, recv_b, hid, acc, dl,
    osend, orecv, fin,
    wsem, ssem, tok_s, tok_r, low_s, low_r, a_s, a_r, b_s, b_r,
    h_s, h_r, p_s, p_r, f_s, f_r, o_s, o_r, z_s, z_r,
):
    n = nt * nd
    half = nd // 2
    depth = wg.shape[0]
    chunk = wgv.shape[2]
    width = wd.shape[1]
    tok_dev = tok.shape[0]
    total_rows = n * tok_dev
    side = total_rows // HALVES
    rows = side // nd
    owners = nd // HALVES
    block = owners * tok_dev
    my_t = lax.axis_index("tensor")
    my_d = lax.axis_index("dp")
    me = my_t * nd + my_d
    my_j = lax.div(my_d, 2)
    my_b = lax.rem(my_d, 2)
    other_b = 1 - my_b
    mate = my_j * 2 + other_b

    def slot_of(t, d):
        return (lax.div(d, owners) * nt + t) * owners + lax.rem(d, owners)

    my_slot = slot_of(my_t, my_d)

    small = [
        pltpu.make_async_copy(tok.at[:, pl.ds(pl.multiple_of(my_d * depth, 128), depth)], xbuf.at[my_slot], ssem.at[0]),
        pltpu.make_async_copy(ag, agv, ssem.at[1]),
        pltpu.make_async_copy(au, auv, ssem.at[2]),
        pltpu.make_async_copy(do.at[:, pl.ds(pl.multiple_of(my_d * width, 128), width)], dov, ssem.at[3]),
    ]

    def cols(ref, c):
        return ref.at[:, c * chunk : (c + 1) * chunk]

    def rows_of(ref, c):
        return ref.at[c * chunk : (c + 1) * chunk, :]

    plan = (
        (wg, wgv, cols), (wu, wuv, cols), (go, gov, cols), (uo, uov, cols),
        (wd, wdv, rows_of), (di, div, cols),
    )

    def load(kind, static_c, c):
        src, dst, cut = plan[kind]
        return pltpu.make_async_copy(cut(src, static_c), dst.at[c], wsem.at[kind, c])

    for copy in small[:3]:
        copy.start()
    for c in range(nc):
        for kind in range(4):
            load(kind, c, c).start()
    barrier = pltpu.get_barrier_semaphore()

    def place(index):
        return {"tensor": lax.div(index, nd), "dp": lax.rem(index, nd)}

    def greet(k, carry):
        pl.semaphore_signal(
            barrier, inc=1, device_id=place(lax.rem(me + k, n)), device_id_type=MESH
        )
        return carry

    lax.fori_loop(1, n, greet, 0)
    pl.semaphore_wait(barrier, n - 1)

    def remote(src, dst, send_sem, recv_sem, device):
        return pltpu.make_async_remote_copy(
            src_ref=src, dst_ref=dst, send_sem=send_sem, recv_sem=recv_sem,
            device_id=device, device_id_type=MESH,
        )

    def tok_copy(k):
        index = lax.rem(me + k, n)
        first = pl.multiple_of(lax.rem(index, nd) * depth, 128)
        return remote(
            tok.at[:, pl.ds(first, depth)], xbuf.at[my_slot],
            tok_s.at[k - 1], tok_r.at[k - 1], place(index),
        )

    def each(low, high, act):
        def step(k, carry):
            act(k)
            return carry

        lax.fori_loop(low, high, step, 0)

    each(1, n, lambda k: tok_copy(k).start())
    small[0].wait()
    each(1, n, lambda k: tok_copy(k).wait_recv())
    for c in range(nc):
        for kind in range(4, 6):
            load(kind, c, c).start()
    small[3].start()
    x[...] = xbuf[...].astype(jnp.float32).reshape(total_rows, depth).astype(jnp.bfloat16)

    small[1].wait()
    small[2].wait()
    for which, ref in ((0, agv), (1, auv)):
        low = dot_rows(x[...], ref[...])
        for d in range(nd):
            for s in range(HALVES):
                first = s * side + d * rows
                lowp[d, which, s] = low[first : first + rows]

    def low_copy(k):
        d = lax.rem(my_d + k, nd)
        return remote(
            lowp.at[d], lowr.at[k - 1], low_s.at[k - 1], low_r.at[k - 1],
            {"tensor": my_t, "dp": d},
        )

    for k in range(1, nd):
        low_copy(k).start()

    def at_dp(d):
        return {"tensor": my_t, "dp": d}

    def a_copy(c):
        return remote(send_a.at[c], recv_a.at[c], a_s.at[c], a_r.at[c], at_dp(mate))

    def ahead(k):
        return lax.rem(my_j + k, half)

    def behind(k):
        return lax.rem(my_j + half - k, half) * 2 + my_b

    def b_copy(c, k):
        return remote(
            send_b.at[c, k - 1], recv_b.at[c, k - 1],
            b_s.at[c, k - 1], b_r.at[c, k - 1], at_dp(ahead(k) * 2 + my_b),
        )

    def h_copy(c, k):
        return remote(
            hid.at[c, my_d], hid.at[c, my_d],
            h_s.at[c, k - 1], h_r.at[c, k - 1], at_dp(ahead(k) * 2 + my_b),
        )

    def p_copy(c):
        return remote(hid.at[c, my_d], hid.at[c, my_d], p_s.at[c], p_r.at[c], at_dp(mate))

    def f_copy(c, k):
        return remote(
            hid.at[c, behind(k)], hid.at[c, behind(k)],
            f_s.at[c, k - 1], f_r.at[c, k - 1], at_dp(mate),
        )

    def rows_at(s, d):
        return pl.ds(pl.multiple_of(s * side + d * rows, rows), rows)

    def up_part(c):
        load(0, 0, c).wait()
        load(1, 0, c).wait()
        part[c, 0] = jnp.dot(x[...], wgv[c], preferred_element_type=jnp.float32)
        part[c, 1] = jnp.dot(x[...], wuv[c], preferred_element_type=jnp.float32)
        for s in range(HALVES):
            for j in range(half):
                for which in range(2):
                    send_a[c, s, j, which] = part[c, which, rows_at(s, 2 * j + other_b), :].astype(
                        jnp.bfloat16
                    )
        a_copy(c).start()

    def pair_sum(q):
        s, c = lax.div(q, nc), lax.rem(q, nc)

        @pl.when(s == 0)
        def _():
            a_copy(c).wait_recv()

        for k in range(1, half):
            j = ahead(k)
            for which in range(2):
                send_b[q, k - 1, which] = (
                    part[c, which, rows_at(s, 2 * j + my_b), :]
                    + recv_a[c, s, j, which].astype(jnp.float32)
                ).astype(jnp.bfloat16)
            b_copy(q, k).start()

    def activate(q):
        s, c = lax.div(q, nc), lax.rem(q, nc)

        @pl.when(q == 0)
        def _():
            for k in range(1, nd):
                low_copy(k).wait_recv()
            total = lowp[my_d]
            for k in range(1, nd):
                total = total + lowr[k - 1]
            lowb[...] = total.astype(jnp.bfloat16)

        @pl.when(s == 0)
        def _():
            load(2, 0, c).wait()
            load(3, 0, c).wait()

        for k in range(1, half):
            b_copy(q, k).wait_recv()
        sums = []
        for which, ref in ((0, gov), (1, uov)):
            value = part[c, which, rows_at(s, my_d), :] + recv_a[c, s, my_j, which].astype(
                jnp.float32
            )
            for k in range(1, half):
                value = value + recv_b[q, k - 1, which].astype(jnp.float32)
            value = value + adapter_scale_factor * jnp.dot(
                lowb[which, s], ref[c], preferred_element_type=jnp.float32
            )
            sums.append(value)
        gate, up = sums
        hid[q, my_d] = (gate / (1.0 + jnp.exp(-gate)) * up).astype(jnp.bfloat16)
        for k in range(1, half):
            h_copy(q, k).start()
        p_copy(q).start()

    def forward(q):
        for k in range(1, half):
            h_copy(q, k).wait_recv()
            f_copy(q, k).start()

    step = 512 if width % 512 == 0 else width

    def down_part(q):
        s, c = lax.div(q, nc), lax.rem(q, nc)

        @pl.when(s == 0)
        def _():
            load(4, 0, c).wait()
            load(5, 0, c).wait()

        p_copy(q).wait_recv()
        for k in range(1, half):
            f_copy(q, k).wait_recv()
        lhs = hid[q].reshape(side, chunk)

        @pl.when(c == 0)
        def _():
            acc[s] = jnp.zeros((side, width), jnp.float32)
            dl[s] = jnp.zeros((side, dl.shape[2]), jnp.float32)

        for first in range(0, width, step):
            acc[s, :, first : first + step] += jnp.dot(
                lhs, wdv[c, :, first : first + step], preferred_element_type=jnp.float32
            )
        dl[s] += dot_rows(lhs, div[c])

        @pl.when(c == nc - 1)
        def _():
            finish(s)

    def finish(s):
        @pl.when(s == 0)
        def _():
            small[3].wait()

        low = dl[s]
        high = low.astype(jnp.bfloat16)
        rest = low - high.astype(jnp.float32)
        middle = rest.astype(jnp.bfloat16)
        last = (rest - middle.astype(jnp.float32)).astype(jnp.bfloat16)
        for first in range(0, width, step):
            maps = dov[:, first : first + step]
            acc[s, :, first : first + step] += adapter_scale_factor * (
                jnp.dot(high, maps, preferred_element_type=jnp.float32)
                + (
                    jnp.dot(middle, maps, preferred_element_type=jnp.float32)
                    + jnp.dot(last, maps, preferred_element_type=jnp.float32)
                )
            )

        def o_send(k):
            osend[s, k - 1] = acc[s, block_at(lax.rem(my_t + k, nt)), :].astype(jnp.bfloat16)
            o_copy(s, k).start()

        each(1, nt, o_send)

    def block_at(t):
        return pl.ds(pl.multiple_of(t * block, block), block)

    def o_copy(s, k):
        t = lax.rem(my_t + k, nt)
        return remote(
            osend.at[s, k - 1], orecv.at[s, k - 1], o_s.at[s, k - 1], o_r.at[s, k - 1],
            {"tensor": t, "dp": my_d},
        )

    mine = pl.ds(pl.multiple_of(my_d * width, 128), width)

    def z_copy(k):
        at = lax.rem(my_d + k, nd)
        return remote(
            fin.at[at], out.at[:, mine], z_s.at[k - 1], z_r.at[k - 1], at_dp(at)
        )

    stages = ((up_part, 0), (pair_sum, SUM_LAG), (activate, ACT_LAG), (forward, FWD_LAG), (down_part, DOWN_LAG))

    def turn(i, carry):
        for stage, lag in stages:
            c = i - lag
            count = nc if stage is up_part else HALVES * nc
            pl.when(jnp.logical_and(c >= 0, c < count))(functools.partial(stage, c))
        return carry

    lax.fori_loop(0, HALVES * nc + DOWN_LAG, turn, 0)

    for s in range(HALVES):
        def o_take(k, s=s):
            o_copy(s, k).wait_recv()
            acc[s, block_at(my_t), :] += orecv[s, k - 1].astype(jnp.float32)

        each(1, nt, o_take)
        fin[s * owners : (s + 1) * owners] = (
            acc[s, block_at(my_t), :].reshape(owners, tok_dev, width).astype(jnp.bfloat16)
        )
    for k in range(1, nd):
        z_copy(k).start()
    out[:, mine] = fin[my_d]

    each(1, n, lambda k: tok_copy(k).wait_send())
    for k in range(1, nd):
        low_copy(k).wait_send()

    def drain(q, carry):
        p_copy(q).wait_send()
        for k in range(1, half):
            b_copy(q, k).wait_send()
            h_copy(q, k).wait_send()
            f_copy(q, k).wait_send()
        return carry

    lax.fori_loop(0, HALVES * nc, drain, 0)
    each(0, nc, lambda c: a_copy(c).wait_send())
    for s in range(HALVES):
        each(1, nt, lambda k, s=s: o_copy(s, k).wait_send())

    def z_wait(k):
        d = lax.rem(my_d + nd - k, nd)
        place_of = pl.ds(pl.multiple_of(d * width, 128), width)
        remote(fin.at[d], out.at[:, place_of], z_s.at[k - 1], z_r.at[k - 1], at_dp(d)).wait_recv()

    for k in range(1, nd):
        z_wait(k)
        z_copy(k).wait_send()


def body(tok, wg, wu, wd, ag, go, au, uo, di, do):
    nt = lax.axis_size("tensor")
    nd = lax.axis_size("dp")
    n = nt * nd
    half = nd // 2
    tok_dev = tok.shape[0]
    depth, hidden = wg.shape
    width = wd.shape[1]
    rank = ag.shape[1]
    chunk = 512 if hidden % 512 == 0 else hidden
    nc = hidden // chunk
    total = n * tok_dev
    side = total // HALVES
    rows = side // nd
    block = nd // HALVES * tok_dev
    items = HALVES * nc
    far = half - 1
    bf, f32 = jnp.bfloat16, jnp.float32
    vm, dma = pltpu.VMEM, pltpu.SemaphoreType.DMA
    scratch = [
        vm((n, tok_dev, depth), bf), vm((total, depth), bf),
        vm((nc, depth, chunk), bf), vm((nc, depth, chunk), bf), vm((nc, chunk, width), bf),
        vm((rank, depth), bf), vm((rank, depth), bf),
        vm((nc, rank, chunk), bf), vm((nc, rank, chunk), bf), vm((nc, rank, chunk), bf),
        vm((rank, width), bf),
        vm((nd, 2, HALVES, rows, rank), f32), vm((nd - 1, 2, HALVES, rows, rank), f32), vm((2, HALVES, rows, rank), bf),
        vm((nc, 2, total, chunk), f32),
        vm((nc, HALVES, half, 2, rows, chunk), bf), vm((nc, HALVES, half, 2, rows, chunk), bf),
        vm((items, far, 2, rows, chunk), bf), vm((items, far, 2, rows, chunk), bf),
        vm((items, nd, rows, chunk), bf),
        vm((HALVES, side, width), f32), vm((HALVES, side, rank), f32),
        vm((HALVES, nt - 1, block, width), bf), vm((HALVES, nt - 1, block, width), bf),
        vm((nd, tok_dev, width), bf),
        dma((6, nc)), dma((4,)), dma((n - 1,)), dma((n - 1,)), dma((nd - 1,)), dma((nd - 1,)),
        dma((nc,)), dma((nc,)), dma((items, far)), dma((items, far)),
        dma((items, far)), dma((items, far)), dma((items,)), dma((items,)),
        dma((items, far)), dma((items, far)),
        dma((HALVES, nt - 1)), dma((HALVES, nt - 1)), dma((nd - 1,)), dma((nd - 1,)),
    ]
    return pl.pallas_call(
        functools.partial(kernel, nt, nd, nc),
        out_shape=jax.ShapeDtypeStruct((tok_dev, width * nd), bf),
        in_specs=[pl.BlockSpec(memory_space=pl.ANY)] * 10,
        out_specs=pl.BlockSpec(memory_space=pltpu.VMEM),
        scratch_shapes=scratch,
        compiler_params=pltpu.CompilerParams(
            collective_id=0, has_side_effects=True, vmem_limit_bytes=67043328
        ),
    )(tok, wg, wu, wd, ag.T, go, au.T, uo, di.T, do)


def solution(mesh):
    placed = (
        P(("groups", "tensor", "dp"), None),
        P("dp", "tensor"),
        P("dp", "tensor"),
        P("tensor", "dp"),
        P(("groups", "dp"), None),
        P(None, ("groups", "tensor")),
        P(("groups", "dp"), None),
        P(None, ("groups", "tensor")),
        P(("groups", "tensor"), None),
        P(None, "groups"),
    )
    return jax.shard_map(
        body,
        mesh=mesh,
        in_specs=placed,
        out_specs=P(("groups", "tensor", "dp"), None),
        check_vma=False,
    )
```

```python
import functools

import jax
import jax.numpy as jnp
from jax import lax
from jax.experimental import pallas as pl
from jax.experimental.pallas import tpu as pltpu
from jax.sharding import PartitionSpec as P

adapter_scale_factor = 0.5
MESH = pl.DeviceIdType.MESH
HALVES = 2
SUM_LAG, ACT_LAG, FWD_LAG, DOWN_LAG = 2, 8, 14, 16


def dot_rows(a, b):
    return lax.dot_general(a, b, (((1,), (1,)), ((), ())), preferred_element_type=jnp.float32)


def kernel(
    nt, nd, nc,
    tok, wg, wu, wd, ag, go, au, uo, di, do, out,
    xbuf, x, wgv, wuv, wdv, agv, auv, gov, uov, div, dov,
    lowp, lowr, lowb, part, send_a, recv_a, send_b, recv_b, hid, acc, dl,
    osend, orecv, fin,
    wsem, ssem, tok_s, tok_r, low_s, low_r, a_s, a_r, b_s, b_r,
    h_s, h_r, p_s, p_r, f_s, f_r, o_s, o_r, z_s, z_r,
):
    n = nt * nd
    half = nd // 2
    depth = wg.shape[0]
    chunk = wgv.shape[2]
    width = wd.shape[1]
    tok_dev = tok.shape[0]
    total_rows = n * tok_dev
    side = total_rows // HALVES
    rows = side // nd
    owners = nd // HALVES
    block = owners * tok_dev
    my_t = lax.axis_index("tensor")
    my_d = lax.axis_index("dp")
    me = my_t * nd + my_d
    my_j = lax.div(my_d, 2)
    my_b = lax.rem(my_d, 2)
    other_b = 1 - my_b
    mate = my_j * 2 + other_b

    def slot_of(t, d):
        return (lax.div(d, owners) * nt + t) * owners + lax.rem(d, owners)

    my_slot = slot_of(my_t, my_d)

    small = [
        pltpu.make_async_copy(tok.at[:, pl.ds(pl.multiple_of(my_d * depth, 128), depth)], xbuf.at[my_slot], ssem.at[0]),
        pltpu.make_async_copy(ag, agv, ssem.at[1]),
        pltpu.make_async_copy(au, auv, ssem.at[2]),
        pltpu.make_async_copy(do.at[:, pl.ds(pl.multiple_of(my_d * width, 128), width)], dov, ssem.at[3]),
    ]

    def cols(ref, c):
        return ref.at[:, c * chunk : (c + 1) * chunk]

    def rows_of(ref, c):
        return ref.at[c * chunk : (c + 1) * chunk, :]

    plan = (
        (wg, wgv, cols), (wu, wuv, cols), (go, gov, cols), (uo, uov, cols),
        (wd, wdv, rows_of), (di, div, cols),
    )

    def load(kind, static_c, c):
        src, dst, cut = plan[kind]
        return pltpu.make_async_copy(cut(src, static_c), dst.at[c], wsem.at[kind, c])

    for copy in small[:3]:
        copy.start()
    for c in range(nc):
        for kind in range(4):
            load(kind, c, c).start()
    barrier = pltpu.get_barrier_semaphore()

    def place(index):
        return {"tensor": lax.div(index, nd), "dp": lax.rem(index, nd)}

    def greet(k, carry):
        pl.semaphore_signal(
            barrier, inc=1, device_id=place(lax.rem(me + k, n)), device_id_type=MESH
        )
        return carry

    lax.fori_loop(1, n, greet, 0)
    pl.semaphore_wait(barrier, n - 1)

    def remote(src, dst, send_sem, recv_sem, device):
        return pltpu.make_async_remote_copy(
            src_ref=src, dst_ref=dst, send_sem=send_sem, recv_sem=recv_sem,
            device_id=device, device_id_type=MESH,
        )

    def tok_copy(k):
        index = lax.rem(me + k, n)
        first = pl.multiple_of(lax.rem(index, nd) * depth, 128)
        return remote(
            tok.at[:, pl.ds(first, depth)], xbuf.at[my_slot],
            tok_s.at[k - 1], tok_r.at[k - 1], place(index),
        )

    def each(low, high, act):
        def step(k, carry):
            act(k)
            return carry

        lax.fori_loop(low, high, step, 0)

    each(1, n, lambda k: tok_copy(k).start())
    small[0].wait()
    each(1, n, lambda k: tok_copy(k).wait_recv())
    for c in range(nc):
        for kind in range(4, 6):
            load(kind, c, c).start()
    small[3].start()
    x[...] = xbuf[...].astype(jnp.float32).reshape(total_rows, depth).astype(jnp.bfloat16)

    small[1].wait()
    small[2].wait()
    for which, ref in ((0, agv), (1, auv)):
        low = dot_rows(x[...], ref[...])
        for d in range(nd):
            for s in range(HALVES):
                first = s * side + d * rows
                lowp[d, which, s] = low[first : first + rows]

    def low_copy(k):
        d = lax.rem(my_d + k, nd)
        return remote(
            lowp.at[d], lowr.at[k - 1], low_s.at[k - 1], low_r.at[k - 1],
            {"tensor": my_t, "dp": d},
        )

    for k in range(1, nd):
        low_copy(k).start()

    def at_dp(d):
        return {"tensor": my_t, "dp": d}

    def a_copy(c):
        return remote(send_a.at[c], recv_a.at[c], a_s.at[c], a_r.at[c], at_dp(mate))

    def ahead(k):
        return lax.rem(my_j + k, half)

    def behind(k):
        return lax.rem(my_j + half - k, half) * 2 + my_b

    def b_copy(c, k):
        return remote(
            send_b.at[c, k - 1], recv_b.at[c, k - 1],
            b_s.at[c, k - 1], b_r.at[c, k - 1], at_dp(ahead(k) * 2 + my_b),
        )

    def h_copy(c, k):
        return remote(
            hid.at[c, my_d], hid.at[c, my_d],
            h_s.at[c, k - 1], h_r.at[c, k - 1], at_dp(ahead(k) * 2 + my_b),
        )

    def p_copy(c):
        return remote(hid.at[c, my_d], hid.at[c, my_d], p_s.at[c], p_r.at[c], at_dp(mate))

    def f_copy(c, k):
        return remote(
            hid.at[c, behind(k)], hid.at[c, behind(k)],
            f_s.at[c, k - 1], f_r.at[c, k - 1], at_dp(mate),
        )

    def rows_at(s, d):
        return pl.ds(pl.multiple_of(s * side + d * rows, rows), rows)

    def up_part(c):
        load(0, 0, c).wait()
        load(1, 0, c).wait()
        part[c, 0] = jnp.dot(x[...], wgv[c], preferred_element_type=jnp.float32)
        part[c, 1] = jnp.dot(x[...], wuv[c], preferred_element_type=jnp.float32)
        for s in range(HALVES):
            for j in range(half):
                for which in range(2):
                    send_a[c, s, j, which] = part[c, which, rows_at(s, 2 * j + other_b), :].astype(
                        jnp.bfloat16
                    )
        a_copy(c).start()

    def pair_sum(q):
        s, c = lax.div(q, nc), lax.rem(q, nc)

        @pl.when(s == 0)
        def _():
            a_copy(c).wait_recv()

        for k in range(1, half):
            j = ahead(k)
            for which in range(2):
                send_b[q, k - 1, which] = (
                    part[c, which, rows_at(s, 2 * j + my_b), :]
                    + recv_a[c, s, j, which].astype(jnp.float32)
                ).astype(jnp.bfloat16)
            b_copy(q, k).start()

    def activate(q):
        s, c = lax.div(q, nc), lax.rem(q, nc)

        @pl.when(q == 0)
        def _():
            for k in range(1, nd):
                low_copy(k).wait_recv()
            total = lowp[my_d]
            for k in range(1, nd):
                total = total + lowr[k - 1]
            lowb[...] = total.astype(jnp.bfloat16)

        @pl.when(s == 0)
        def _():
            load(2, 0, c).wait()
            load(3, 0, c).wait()

        for k in range(1, half):
            b_copy(q, k).wait_recv()
        sums = []
        for which, ref in ((0, gov), (1, uov)):
            value = part[c, which, rows_at(s, my_d), :] + recv_a[c, s, my_j, which].astype(
                jnp.float32
            )
            for k in range(1, half):
                value = value + recv_b[q, k - 1, which].astype(jnp.float32)
            value = value + adapter_scale_factor * jnp.dot(
                lowb[which, s], ref[c], preferred_element_type=jnp.float32
            )
            sums.append(value)
        gate, up = sums
        hid[q, my_d] = (gate / (1.0 + jnp.exp(-gate)) * up).astype(jnp.bfloat16)
        for k in range(1, half):
            h_copy(q, k).start()
        p_copy(q).start()

    def forward(q):
        for k in range(1, half):
            h_copy(q, k).wait_recv()
            f_copy(q, k).start()

    step = 512 if width % 512 == 0 else width

    def down_part(q):
        s, c = lax.div(q, nc), lax.rem(q, nc)

        @pl.when(s == 0)
        def _():
            load(4, 0, c).wait()
            load(5, 0, c).wait()

        p_copy(q).wait_recv()
        for k in range(1, half):
            f_copy(q, k).wait_recv()
        lhs = hid[q].reshape(side, chunk)

        @pl.when(c == 0)
        def _():
            acc[s] = jnp.zeros((side, width), jnp.float32)
            dl[s] = jnp.zeros((side, dl.shape[2]), jnp.float32)

        for first in range(0, width, step):
            acc[s, :, first : first + step] += jnp.dot(
                lhs, wdv[c, :, first : first + step], preferred_element_type=jnp.float32
            )
        dl[s] += dot_rows(lhs, div[c])

        @pl.when(c == nc - 1)
        def _():
            finish(s)

    def finish(s):
        @pl.when(s == 0)
        def _():
            small[3].wait()

        low = dl[s]
        high = low.astype(jnp.bfloat16)
        rest = low - high.astype(jnp.float32)
        middle = rest.astype(jnp.bfloat16)
        last = (rest - middle.astype(jnp.float32)).astype(jnp.bfloat16)
        for first in range(0, width, step):
            maps = dov[:, first : first + step]
            acc[s, :, first : first + step] += adapter_scale_factor * (
                jnp.dot(high, maps, preferred_element_type=jnp.float32)
                + (
                    jnp.dot(middle, maps, preferred_element_type=jnp.float32)
                    + jnp.dot(last, maps, preferred_element_type=jnp.float32)
                )
            )

        def o_send(k):
            osend[s, k - 1] = acc[s, block_at(lax.rem(my_t + k, nt)), :].astype(jnp.bfloat16)
            o_copy(s, k).start()

        each(1, nt, o_send)

    def block_at(t):
        return pl.ds(pl.multiple_of(t * block, block), block)

    def o_copy(s, k):
        t = lax.rem(my_t + k, nt)
        return remote(
            osend.at[s, k - 1], orecv.at[s, k - 1], o_s.at[s, k - 1], o_r.at[s, k - 1],
            {"tensor": t, "dp": my_d},
        )

    mine = pl.ds(pl.multiple_of(my_d * width, 128), width)

    def z_copy(k):
        at = lax.rem(my_d + k, nd)
        return remote(
            fin.at[at], out.at[:, mine], z_s.at[k - 1], z_r.at[k - 1], at_dp(at)
        )

    stages = ((up_part, 0), (pair_sum, SUM_LAG), (activate, ACT_LAG), (forward, FWD_LAG), (down_part, DOWN_LAG))

    def turn(i, carry):
        for stage, lag in stages:
            c = i - lag
            count = nc if stage is up_part else HALVES * nc
            pl.when(jnp.logical_and(c >= 0, c < count))(functools.partial(stage, c))
        return carry

    lax.fori_loop(0, HALVES * nc + DOWN_LAG, turn, 0)

    for s in range(HALVES):
        def o_take(k, s=s):
            o_copy(s, k).wait_recv()
            acc[s, block_at(my_t), :] += orecv[s, k - 1].astype(jnp.float32)

        each(1, nt, o_take)
        fin[s * owners : (s + 1) * owners] = (
            acc[s, block_at(my_t), :].reshape(owners, tok_dev, width).astype(jnp.bfloat16)
        )
    for k in range(1, nd):
        z_copy(k).start()
    out[:, mine] = fin[my_d]

    each(1, n, lambda k: tok_copy(k).wait_send())
    for k in range(1, nd):
        low_copy(k).wait_send()

    def drain(q, carry):
        p_copy(q).wait_send()
        for k in range(1, half):
            b_copy(q, k).wait_send()
            h_copy(q, k).wait_send()
            f_copy(q, k).wait_send()
        return carry

    lax.fori_loop(0, HALVES * nc, drain, 0)
    each(0, nc, lambda c: a_copy(c).wait_send())
    for s in range(HALVES):
        each(1, nt, lambda k, s=s: o_copy(s, k).wait_send())

    def z_wait(k):
        d = lax.rem(my_d + nd - k, nd)
        place_of = pl.ds(pl.multiple_of(d * width, 128), width)
        remote(fin.at[d], out.at[:, place_of], z_s.at[k - 1], z_r.at[k - 1], at_dp(d)).wait_recv()

    for k in range(1, nd):
        z_wait(k)
        z_copy(k).wait_send()


def body(tok, wg, wu, wd, ag, go, au, uo, di, do):
    nt = lax.axis_size("tensor")
    nd = lax.axis_size("dp")
    n = nt * nd
    half = nd // 2
    tok_dev = tok.shape[0]
    depth, hidden = wg.shape
    width = wd.shape[1]
    rank = ag.shape[1]
    chunk = 512 if hidden % 512 == 0 else hidden
    nc = hidden // chunk
    total = n * tok_dev
    side = total // HALVES
    rows = side // nd
    block = nd // HALVES * tok_dev
    items = HALVES * nc
    far = half - 1
    bf, f32 = jnp.bfloat16, jnp.float32
    vm, dma = pltpu.VMEM, pltpu.SemaphoreType.DMA
    scratch = [
        vm((n, tok_dev, depth), bf), vm((total, depth), bf),
        vm((nc, depth, chunk), bf), vm((nc, depth, chunk), bf), vm((nc, chunk, width), bf),
        vm((rank, depth), bf), vm((rank, depth), bf),
        vm((nc, rank, chunk), bf), vm((nc, rank, chunk), bf), vm((nc, rank, chunk), bf),
        vm((rank, width), bf),
        vm((nd, 2, HALVES, rows, rank), f32), vm((nd - 1, 2, HALVES, rows, rank), f32), vm((2, HALVES, rows, rank), bf),
        vm((nc, 2, total, chunk), f32),
        vm((nc, HALVES, half, 2, rows, chunk), bf), vm((nc, HALVES, half, 2, rows, chunk), bf),
        vm((items, far, 2, rows, chunk), bf), vm((items, far, 2, rows, chunk), bf),
        vm((items, nd, rows, chunk), bf),
        vm((HALVES, side, width), f32), vm((HALVES, side, rank), f32),
        vm((HALVES, nt - 1, block, width), bf), vm((HALVES, nt - 1, block, width), bf),
        vm((nd, tok_dev, width), bf),
        dma((6, nc)), dma((4,)), dma((n - 1,)), dma((n - 1,)), dma((nd - 1,)), dma((nd - 1,)),
        dma((nc,)), dma((nc,)), dma((items, far)), dma((items, far)),
        dma((items, far)), dma((items, far)), dma((items,)), dma((items,)),
        dma((items, far)), dma((items, far)),
        dma((HALVES, nt - 1)), dma((HALVES, nt - 1)), dma((nd - 1,)), dma((nd - 1,)),
    ]
    return pl.pallas_call(
        functools.partial(kernel, nt, nd, nc),
        out_shape=jax.ShapeDtypeStruct((tok_dev, width * nd), bf),
        in_specs=[pl.BlockSpec(memory_space=pl.ANY)] * 10,
        out_specs=pl.BlockSpec(memory_space=pltpu.VMEM),
        scratch_shapes=scratch,
        compiler_params=pltpu.CompilerParams(
            collective_id=0, has_side_effects=True, vmem_limit_bytes=67043328
        ),
    )(tok, wg, wu, wd, ag.T, go, au.T, uo, di.T, do)


def solution(mesh):
    placed = (
        P(("groups", "tensor", "dp"), None),
        P("dp", "tensor"),
        P("dp", "tensor"),
        P("tensor", "dp"),
        P(("groups", "dp"), None),
        P(None, ("groups", "tensor")),
        P(("groups", "dp"), None),
        P(None, ("groups", "tensor")),
        P(("groups", "tensor"), None),
        P(None, "groups"),
    )
    return jax.shard_map(
        body,
        mesh=mesh,
        in_specs=placed,
        out_specs=P(("groups", "tensor", "dp"), None),
        check_vma=False,
    )
```
